32 devices in a mesh: groups: 2 (over y), tok: 4 (over x, core), head: 4 (over z).
Axes of the slice: x: 2, y: 2, z: 4, core: 2. Of those that a mesh axis runs over, the one named last changes fastest.
Arguments:
- keys: bfloat16 [24576, 1280], P(('groups', 'tok'), 'head'), parts along dimension 0, may hold values from -6 to 6
- values: bfloat16 [24576, 1280], P(('groups', 'tok'), 'head'), parts along dimension 0, may hold values from -6 to 6
- rates: float32 [24576, 4], P(('groups', 'tok'), 'head'), parts along dimension 0, may hold values from 0.5 to 4
- fast_init: bfloat16 [4, 3, 320, 320], P('head'), may hold values from -6 to 6
- samples: bfloat16 [512, 5120], P('groups', 'tok'), parts along dimension 0, may hold values from -6 to 6
- w_query: bfloat16 [5120, 1280], P('tok', 'head'), may hold values from -0.078125 to 0.078125
- w_output: bfloat16 [1280, 5120], P('head', 'tok'), may hold values from -0.15625 to 0.15625
Outputs:
- mixed: bfloat16 [512, 5120], P(('groups', 'head'), 'tok'), parts along dimension 0
- fast_new: bfloat16 [8, 3, 320, 320], P(('groups', 'head')), parts along dimension 0
The draws below stay inside these ranges and needn't reach their ends.
There are 2 independent parts, one for each index of `groups`. The reference program is written for one: setup_inputs(seed, part) draws one part's arguments, and reference() takes and returns one part's arrays. A program takes and returns all parts, laid end to end along the dimension named above; an argument that names none is the same for every part. Nothing has to cross between parts.
All inputs are finite; a program needn't handle non-finite values.
Results may differ from the reference program's by a relative error of at most 0.012.
Values may be sent and summed in bfloat16 or wider, within the bound.
A program may use at most 64 MiB of HBM per device.

```python
import math
import jax
import jax.numpy as jnp
from jax import lax

D = 5120
HD = 320
HEADS = 4
PROMPT = 12288
SAMPLES = 256


def steps_of(key, extent, split, smallest, high):
    def one(axis_at, shards_of):
        heights = jax.random.uniform(jax.random.fold_in(jax.random.fold_in(key, 6), axis_at), (shards_of,), jnp.float32, smallest / len(split), high / len(split))
        return jnp.repeat(jnp.exp(heights), extent[axis_at] // shards_of).reshape((-1,) + (1,) * (len(extent) - axis_at - 1))

    factor_of = one(*split[0])
    for cut in split[1:]:
        factor_of = factor_of * one(*cut)
    return factor_of


def centred(stream_key, dims, scale, limit, cuts=(), held_as=jnp.bfloat16):
    level = steps_of(stream_key, dims, cuts, -0.22, 0.18) if cuts else 1.0
    result = jax.random.normal(stream_key, dims, jnp.float32) * scale * level
    return jnp.minimum(jnp.maximum(result, -limit), limit).astype(held_as)


def setup_inputs(seed: int = 0, part: int = 0) -> dict:
    splits = jax.random.split(jax.random.key(seed), 8)
    part_keys = jax.random.split(jax.random.fold_in(splits[7], part), 8)
    keys = centred(part_keys[0], (PROMPT, HEADS * HD), 1.0, 6.0, ((0, 4), (1, 4)))
    values = centred(part_keys[1], (PROMPT, HEADS * HD), 1.0, 6.0, ((0, 4), (1, 4)))
    rates = jnp.clip(jnp.exp(math.log(4.0) - 2.0794415 * jax.random.uniform(part_keys[2], (PROMPT, HEADS), jnp.float32) ** steps_of(part_keys[2], (PROMPT, HEADS), ((0, 4), (1, 4)), -0.2, 0.2)), 0.5, 4.0)
    fast_init = centred(splits[3], (HEADS, 3, HD, HD), 1.0, 6.0, ((0, 4),))
    samples = centred(part_keys[4], (SAMPLES, D), 1.0, 6.0, ((1, 4),))
    w_query = centred(splits[5], (D, HEADS * HD), D ** -0.5, 0.078125, ((0, 4), (1, 4)))
    w_output = centred(splits[6], (HEADS * HD, D), (HEADS * HD) ** -0.5, 0.15625, ((0, 4), (1, 4)))
    return dict(keys=keys, values=values, rates=rates, fast_init=fast_init, samples=samples, w_query=w_query, w_output=w_output)


def unit_rows(block):
    wide = block.astype(jnp.float32)
    return (wide * lax.rsqrt(lax.optimization_barrier(jnp.sum(wide * wide, axis=-1, keepdims=True)) + 1e-06)).astype(jnp.bfloat16)

def head_gradient(operands):
    head_keys, head_values, head_rates, weights = operands
    normed = unit_rows(head_keys)
    pre_gate = jnp.dot(normed, weights[0], preferred_element_type=jnp.float32)
    pre_up = jnp.dot(normed, weights[1], preferred_element_type=jnp.float32)
    gate_sigmoid = jax.nn.sigmoid(pre_gate)
    activated = pre_gate * gate_sigmoid
    hidden = (activated * pre_up).astype(jnp.bfloat16)
    scaled = (head_rates[:, None] * head_values.astype(jnp.float32)).astype(jnp.bfloat16)
    hidden_grad = jnp.dot(scaled, weights[2].T, preferred_element_type=jnp.float32)
    gate_grad = (hidden_grad * pre_up * gate_sigmoid * (1.0 + pre_gate * (1.0 - gate_sigmoid))).astype(jnp.bfloat16)
    up_grad = (hidden_grad * activated).astype(jnp.bfloat16)
    first = jnp.dot(normed.T, gate_grad, preferred_element_type=jnp.float32)
    second = jnp.dot(normed.T, up_grad, preferred_element_type=jnp.float32)
    third = jnp.dot(hidden.T, scaled, preferred_element_type=jnp.float32)
    return jnp.stack([first, second, third])

def renorm(weights, gradient):
    former = weights.astype(jnp.float32)
    updated = former + gradient
    factor = jnp.sqrt((lax.optimization_barrier(jnp.mean(former * former, axis=-1, keepdims=True)) + 1e-05) / (lax.optimization_barrier(jnp.mean(updated * updated, axis=-1, keepdims=True)) + 1e-05))
    return (updated * factor).astype(jnp.bfloat16)

def fast_apply(normed, weights):
    wide = normed.astype(jnp.float32)
    sample_gate = jnp.einsum('shd,hde->she', wide, weights[:, 0].astype(jnp.float32))
    sample_up = jnp.einsum('shd,hde->she', wide, weights[:, 1].astype(jnp.float32))
    sample_hidden = (jax.nn.silu(sample_gate) * sample_up).astype(jnp.bfloat16)
    fast_out = jnp.einsum('shd,hde->she', sample_hidden.astype(jnp.float32), weights[:, 2].astype(jnp.float32))
    return (fast_out * lax.rsqrt(lax.optimization_barrier(jnp.mean(fast_out * fast_out, axis=-1, keepdims=True)) + 1e-05)).astype(jnp.bfloat16)

def reference(keys, values, rates, fast_init, samples, w_query, w_output):
    head_keys = jnp.moveaxis(keys.reshape(PROMPT, HEADS, HD), 1, 0)
    head_values = jnp.moveaxis(values.reshape(PROMPT, HEADS, HD), 1, 0)
    gradient = lax.map(head_gradient, (head_keys, head_values, rates.T, fast_init))
    gradient = gradient * PROMPT ** (-0.5)
    fast_new = renorm(fast_init, gradient)
    queries = jnp.dot(samples, w_query, preferred_element_type=jnp.float32)
    normed_queries = unit_rows(queries.reshape(SAMPLES, HEADS, HD))
    normed_out = fast_apply(normed_queries, fast_new)
    mixed = jnp.dot(normed_out.reshape(SAMPLES, HEADS * HD), w_output, preferred_element_type=jnp.float32)
    return (mixed.astype(jnp.bfloat16), fast_new)
```

```python
import functools

import jax
import jax.numpy as jnp
from jax import lax
from jax.experimental import pallas as pl
from jax.experimental.pallas import tpu as pltpu
from jax.sharding import PartitionSpec as P

MESH = pl.DeviceIdType.MESH
F32 = jnp.float32
BF16 = jnp.bfloat16


def dot(a, b):
    return jnp.dot(a, b, preferred_element_type=F32)


def dot_tn(a, b):
    return lax.dot_general(a, b, (((0,), (0,)), ((), ())), preferred_element_type=F32)


def dot_nt(a, b):
    return lax.dot_general(a, b, (((1,), (1,)), ((), ())), preferred_element_type=F32)


def sigmoid(v):
    return 0.5 * jnp.tanh(0.5 * v) + 0.5


def pack(block):
    r, hd = block.shape
    full = hd // 128
    parts = [block[:, 128 * i : 128 * (i + 1)] for i in range(full)]
    tail = block[:, 128 * full :]
    parts.append(jnp.concatenate([tail[: r // 2], tail[r // 2 :]], axis=1))
    return parts


def unpack(rows_of, r, hd):
    full = hd // 128
    parts = [rows_of(i * r, r) for i in range(full)]
    tail = rows_of(full * r, r // 2)
    parts.append(jnp.concatenate([tail[:, :64], tail[:, 64:]], axis=0))
    return jnp.concatenate(parts, axis=1)


def kernel(
    n_group, n_tok, n_head, far, n_long, chunks, step_scale,
    keys_h, values_h, rates_h, init_h, samples_h, wq_h, wo_h,
    mixed_ref, fnew,
    keys_v, values_v, rates_v, init_v, samples_v, wq_v, wo_v, wo_near, wo_far,
    w13, normed_v, scaled_v, hidden_v, act_v, slope_v, gate_v, up_v, acc, crecv, xbuf,
    qbuf, qpeer, qx, nq, nout, nrecv, nfar, own_t, far_t, tsend, trecv, dsend, drecv,
    load_sem, chunk_sem, ssem, rsem,
):
    g = lax.axis_index("groups")
    t = lax.axis_index("tok")
    h = lax.axis_index("head")
    n_x = n_tok // 2
    n_pair = n_head // 2
    x = t // 2
    core = lax.rem(t, 2)
    par = lax.rem(h, 2)
    pair = h // 2
    core_peer = {"tok": 2 * x + 1 - core}
    head_peer = {"head": 2 * pair + 1 - par}
    x_peers = [{"tok": 2 * lax.rem(x + d, n_x) + core} for d in range(1, n_x)]
    g_peers = [{"groups": lax.rem(g + d, n_group)} for d in range(1, n_group)]
    pair_of = [lax.rem(pair + o, n_pair) for o in range(n_pair)]
    par_peers = [{"head": 2 * pair_of[o] + par} for o in range(1, n_pair)]

    barrier = pltpu.get_barrier_semaphore()
    everyone = [core_peer, head_peer] + x_peers + g_peers + par_peers
    for peer in everyone:
        pl.semaphore_signal(barrier, inc=1, device_id=peer, device_id_type=MESH)

    sends, held = [], {}
    short = ssem.shape[0] - n_long

    def send(src, dst, peer, long=False):
        turn = sum(1 for c in sends if c[1] == long)
        slot = short + turn if long else turn % short
        if slot in held:
            held[slot].wait_send()
        copy = pltpu.make_async_remote_copy(
            src_ref=src, dst_ref=dst, send_sem=ssem.at[slot], recv_sem=rsem.at[len(sends)],
            device_id=peer, device_id_type=MESH,
        )
        copy.start()
        held[slot] = copy
        sends.append((copy, long))
        return copy

    rows = keys_h.shape[1] // chunks

    def chunk_at(i):
        return pl.ds(i * rows, rows)

    key_loads = [
        pltpu.make_async_copy(
            keys_h.at[:, chunk_at(i)], keys_v.at[:, chunk_at(i)], chunk_sem.at[0, i])
        for i in range(chunks)
    ]
    value_loads = [
        pltpu.make_async_copy(
            values_h.at[:, chunk_at(i)], values_v.at[:, chunk_at(i)], chunk_sem.at[1, i])
        for i in range(chunks)
    ]
    loads = [
        pltpu.make_async_copy(samples_h, samples_v, load_sem.at[0]),
        pltpu.make_async_copy(wq_h, wq_v, load_sem.at[1]),
        pltpu.make_async_copy(init_h.at[0], init_v, load_sem.at[2]),
        pltpu.make_async_copy(rates_h, rates_v, load_sem.at[3]),
        pltpu.make_async_copy(wo_h, wo_v, load_sem.at[4]),
    ]
    for load in loads[:4]:
        load.start()
    for i in range(chunks):
        key_loads[i].start()
        value_loads[i].start()
    loads[4].start()

    hd = fnew.shape[2]
    half = hd // 2
    qrows = qbuf.shape[1]
    group = nq.shape[2]
    cols = wo_h.shape[1]
    near = cols - far

    loads[0].wait()
    loads[1].wait()
    queries = dot_nt(samples_v[...], wq_v[...])
    qbuf[0] = queries[:qrows]
    qbuf[1] = queries[qrows:]
    loads[2].wait()
    w13[:hd] = init_v[0].T
    w13[hd:] = init_v[1].T

    pl.semaphore_wait(barrier, len(everyone))

    q_core = send(qbuf.at[1 - core], qpeer, core_peer)

    share = hd // n_group
    first = pl.multiple_of(share * g, 16)
    w_in = []
    if far:
        step = share // 2 if share % 32 == 0 else share
        for r in range(0, share, step):
            at = pl.ds(first + r, step)
            w_in.append((
                send(wo_h.at[at, pl.ds(0, far)], wo_far.at[at], par_peers[0], True), wo_far.at[at]))
    at = pl.ds(first, share)
    w_in.append((
        send(wo_h.at[at, pl.ds(far, near)], wo_near.at[at], head_peer, True), wo_near.at[at]))
    passed = []

    def pass_on(n):
        for _ in range(min(n, len(w_in))):
            copy, ref = w_in.pop(0)
            copy.wait_recv()
            for peer in g_peers:
                passed.append(send(ref, ref, peer, True))

    loads[3].wait()

    def store_packed(ref, lead, block):
        at = 0
        for part in pack(block):
            ref[lead + (slice(at, at + part.shape[0]),)] = part
            at += part.shape[0]

    q_x = []
    for i in range(chunks):
        key_loads[i].wait()
        value_loads[i].wait()
        at = chunk_at(i)
        k = keys_v[:, at].astype(F32)
        normed = (k * lax.rsqrt(jnp.sum(k * k, axis=0, keepdims=True) + 1e-06)).astype(BF16)
        normed_v[:, at] = normed
        pre = dot(w13[...], normed)
        gate, up = pre[:hd], pre[hd:]
        scaled_v[:, at] = (rates_v[:, at] * values_v[:, at].astype(F32)).astype(BF16)
        s = sigmoid(gate)
        a = gate * s
        hidden_v[:, at] = (a * up).astype(BF16)
        act_v[:, at] = a
        slope_v[:, at] = up * (s + a * (1.0 - s))
        if i == 0:
            q_core.wait_recv()
            store_packed(qx, (x,), (qbuf[core] + qpeer[...]).astype(BF16))
            for peer in x_peers:
                q_x.append(send(qx.at[x], qx.at[x], peer))

    theirs = pl.ds(pl.multiple_of(half * (1 - core), half), half)
    mine = pl.ds(pl.multiple_of(half * core, half), half)
    c_copies, x_copies = {}, {}

    def partial(m, a, b):
        acc[m] = dot_nt(a[...], b[...])
        c_copies[m] = send(acc.at[m, theirs], crecv.at[m], core_peer)

    def chip_sum(m):
        c_copies[m].wait_recv()
        store_packed(xbuf, (m, x), (acc[m, mine, :] + crecv[m]).astype(BF16))
        x_copies[m] = [send(xbuf.at[m, x], xbuf.at[m, x], peer) for peer in x_peers]

    partial(2, hidden_v, scaled_v)
    for i in range(chunks):
        at = chunk_at(i)
        hidden_grad = dot(init_v[2], scaled_v[:, at])
        up_v[:, at] = (hidden_grad * act_v[:, at]).astype(BF16)
        gate_v[:, at] = (hidden_grad * slope_v[:, at]).astype(BF16)
        if i == chunks - 2:
            chip_sum(2)
    partial(1, normed_v, up_v)
    partial(0, normed_v, gate_v)
    chip_sum(1)

    for c in q_x:
        c.wait_recv()

    def unpack_of(ref, lead, r):
        return unpack(lambda at, n: ref[lead + (slice(at, at + n),)].astype(F32), r, hd)

    queries = unpack_of(qx, (0,), qrows)
    for j in range(1, n_x):
        queries = queries + unpack_of(qx, (j,), qrows)
    normed_q = (
        queries * lax.rsqrt(jnp.sum(queries * queries, axis=-1, keepdims=True) + 1e-06)
    ).astype(BF16)
    for j in range(nq.shape[1]):
        nq[core, j] = normed_q[j * group : (j + 1) * group]
    q_last = send(nq.at[core], nq.at[core], core_peer)
    chip_sum(0)
    pass_on(1)

    f_copies = {}

    def renorm(m):
        for c in x_copies[m]:
            c.wait_recv()
        total = unpack_of(xbuf, (m, 0), half)
        for j in range(1, n_x):
            total = total + unpack_of(xbuf, (m, j), half)
        former = init_v[m, mine, :].astype(F32)
        updated = former + total * step_scale
        factor = jnp.sqrt(
            (jnp.mean(former * former, axis=-1, keepdims=True) + 1e-05)
            / (jnp.mean(updated * updated, axis=-1, keepdims=True) + 1e-05)
        )
        fnew[0, m, mine, :] = (updated * factor).astype(BF16)
        f_copies[m] = send(fnew.at[0, m, mine], fnew.at[0, m, mine], core_peer)

    order = list(range(1, n_pair)) + [0]
    per_half = nq.shape[1]
    block = group // 2
    renorm(2)
    q_last.wait_recv()
    renorm(1)
    pass_on(len(w_in))
    normed_q = [nq[pair_of[o] // per_half, lax.rem(pair_of[o], per_half)] for o in order]
    f_copies[2].wait_recv()
    f_copies[1].wait_recv()
    ups = [dot(rows_q, fnew[0, 1]) for rows_q in normed_q]
    renorm(0)
    loads[4].wait()
    f_copies[0].wait_recv()
    hiddens = []
    for up, rows_q in zip(ups, normed_q):
        gate = dot(rows_q, fnew[0, 0])
        hiddens.append((gate * sigmoid(gate) * up).astype(BF16))
    n_copies = {}
    for o, sample_hidden in zip(order, hiddens):
        fast_out = dot(sample_hidden, fnew[0, 2])
        normed_out = (
            fast_out * lax.rsqrt(jnp.mean(fast_out * fast_out, axis=-1, keepdims=True) + 1e-05)
        ).astype(BF16)
        nout[o, 0] = normed_out[:block]
        nout[o, 1] = normed_out[block:]
        if far and o:
            n_far = send(nout.at[o, core], nfar.at[core], par_peers[0])
        n_copies[o] = send(nout.at[o, 1 - par], nrecv.at[o], head_peer)

    for o in order:
        own_t[o] = dot(nout[o, par], wo_v[:, far:])
    if far:
        for q in range(2):
            far_t[q] = dot(nout[0, q], wo_v[:, :far])
    if far:
        n_far.wait_recv()
        n_core = send(nfar.at[core], nfar.at[core], core_peer)
    for copy in passed:
        copy.wait_recv()
    t_copies = {}
    for o in range(1, n_pair):
        n_copies[o].wait_recv()
        tsend[o - 1] = (own_t[o] + dot(nrecv[o], wo_near[...])).astype(BF16)
        t_copies[o] = send(tsend.at[o - 1], trecv.at[o - 1], par_peers[o - 1])
    if far:
        n_core.wait_recv()
        dsend[...] = (far_t[1 - par] + dot(nfar[1 - par], wo_far[...])).astype(BF16)
        d_copy = send(dsend, drecv, head_peer)
        far_sum = far_t[par] + dot(nfar[par], wo_far[...])
    n_copies[0].wait_recv()
    mixed = own_t[0] + dot(nrecv[0], wo_near[...])
    if far:
        d_copy.wait_recv()
        mixed_ref[:, :far] = (far_sum + drecv[...].astype(F32)).astype(BF16)
    for o in range(1, n_pair):
        t_copies[o].wait_recv()
        mixed = mixed + trecv[o - 1].astype(F32)
    mixed_ref[:, far:] = mixed.astype(BF16)

    for c in held.values():
        c.wait_send()


def copy_out(mixed_v, fast_v, mixed_out, fast_out, sem):
    stores = [
        pltpu.make_async_copy(fast_v, fast_out, sem.at[0]),
        pltpu.make_async_copy(mixed_v, mixed_out, sem.at[1]),
    ]
    for c in stores:
        c.start()
    for c in stores:
        c.wait()


FAR = 896


def shards(n_group, n_tok, n_head, keys, values, rates, fast_init, samples, w_query, w_output):
    tokens = keys.shape[0]
    hd = fast_init.shape[2]
    chunks = 3
    srows = samples.shape[0]
    block = srows // n_head
    cols = w_output.shape[1]
    n_x, n_pair = n_tok // 2, n_head // 2
    far = FAR if n_pair == 2 else 0
    near = cols - far
    dma = pltpu.SemaphoreType.DMA
    others = max(n_pair - 1, 1)
    anywhere = pl.BlockSpec(memory_space=pl.ANY)
    vmem = pltpu.VMEM
    in_vmem = pl.BlockSpec(memory_space=vmem)
    packed = (hd // 2) * hd // 128
    qrows = srows // 2
    weights = (2 if far and (hd // n_group) % 32 == 0 else 1 if far else 0) + 1
    n_long = weights * n_group
    n_sem = 8 + 4 * (n_x - 1) + 2 * n_pair - 1 + (3 if far else 0) + n_long
    body = functools.partial(
        kernel, n_group, n_tok, n_head, far, n_long, chunks, float(tokens * n_tok) ** (-0.5)
    )
    mixed, fast_new = pl.pallas_call(
        body,
        out_shape=(vmem((block, cols), BF16), vmem((1, 3, hd, hd), BF16)),
        in_specs=[anywhere] * 7,
        out_specs=(in_vmem, in_vmem),
        scratch_shapes=[
            vmem((hd, tokens), BF16),
            vmem((hd, tokens), BF16),
            vmem((1, tokens), F32),
            vmem((3, hd, hd), BF16),
            vmem(samples.shape, BF16),
            vmem((hd, w_query.shape[0]), BF16),
            vmem(w_output.shape, BF16),
            vmem((hd, near), BF16),
            vmem((hd, far or 128), BF16),
            vmem((2 * hd, hd), BF16),
            vmem((hd, tokens), BF16),
            vmem((hd, tokens), BF16),
            vmem((hd, tokens), BF16),
            vmem((hd, tokens), F32),
            vmem((hd, tokens), F32),
            vmem((hd, tokens), BF16),
            vmem((hd, tokens), BF16),
            vmem((3, hd, hd), F32),
            vmem((3, hd // 2, hd), F32),
            vmem((3, n_x, packed, 128), BF16),
            vmem((2, qrows, hd), F32),
            vmem((qrows, hd), F32),
            vmem((n_x, qrows * hd // 128, 128), BF16),
            vmem((2, n_pair // 2, 2 * block, hd), BF16),
            vmem((n_pair, 2, block, hd), BF16),
            vmem((n_pair, block, hd), BF16),
            vmem((2, block, hd), BF16),
            vmem((n_pair, block, near), F32),
            vmem((2, block, far or 128), F32),
            vmem((others, block, near), BF16),
            vmem((others, block, near), BF16),
            vmem((block, far or 128), BF16),
            vmem((block, far or 128), BF16),
            dma((5,)),
            dma((2, chunks)),
            dma((6 + n_long,)),
            dma((n_sem,)),
        ],
        compiler_params=pltpu.CompilerParams(
            collective_id=0, has_side_effects=True, vmem_limit_bytes=60 << 20
        ),
    )(keys.T, values.T, rates.T, fast_init, samples, w_query.T, w_output)
    outs = (
        jax.ShapeDtypeStruct((block, cols), BF16),
        jax.ShapeDtypeStruct((1, 3, hd, hd), BF16),
    )
    return pl.pallas_call(
        copy_out,
        out_shape=outs,
        in_specs=[in_vmem] * 2,
        out_specs=(anywhere, anywhere),
        scratch_shapes=[dma((2,))],
    )(
        pltpu.with_memory_space_constraint(mixed, vmem),
        pltpu.with_memory_space_constraint(fast_new, vmem),
    )


def solution(mesh):
    return jax.shard_map(
        functools.partial(
            shards, mesh.shape["groups"], mesh.shape["tok"], mesh.shape["head"]
        ),
        mesh=mesh,
        in_specs=(
            P(("groups", "tok"), "head"),
            P(("groups", "tok"), "head"),
            P(("groups", "tok"), "head"),
            P("head", None, None, None),
            P("groups", "tok"),
            P("tok", "head"),
            P("head", "tok"),
        ),
        out_specs=(P(("groups", "head"), "tok"), P(("groups", "head"), None, None, None)),
        check_vma=False,
    )
```

```python
import functools

import jax
import jax.numpy as jnp
from jax import lax
from jax.experimental import pallas as pl
from jax.experimental.pallas import tpu as pltpu
from jax.sharding import PartitionSpec as P

MESH = pl.DeviceIdType.MESH
F32 = jnp.float32
BF16 = jnp.bfloat16


def dot(a, b):
    return jnp.dot(a, b, preferred_element_type=F32)


def dot_tn(a, b):
    return lax.dot_general(a, b, (((0,), (0,)), ((), ())), preferred_element_type=F32)


def dot_nt(a, b):
    return lax.dot_general(a, b, (((1,), (1,)), ((), ())), preferred_element_type=F32)


def sigmoid(v):
    return 0.5 * jnp.tanh(0.5 * v) + 0.5


def pack(block):
    r, hd = block.shape
    full = hd // 128
    parts = [block[:, 128 * i : 128 * (i + 1)] for i in range(full)]
    if hd % 128:
        tail = block[:, 128 * full :]
        parts.append(jnp.concatenate([tail[: r // 2], tail[r // 2 :]], axis=1))
    return parts


def unpack(rows_of, r, hd):
    full = hd // 128
    parts = [rows_of(i * r, r) for i in range(full)]
    tail = rows_of(full * r, r // 2)
    parts.append(jnp.concatenate([tail[:, :64], tail[:, 64:]], axis=0))
    return jnp.concatenate(parts, axis=1)


def kernel(
    n_group, n_tok, n_head, far, n_long, chunks, step_scale,
    keys_h, values_h, rates_h, init_h, samples_h, wq_h, wo_h,
    mixed_ref, fnew,
    keys_v, values_v, rates_v, init_v, samples_v, wq_v, wo_v, wo_near, wo_far,
    w13, normed_v, scaled_v, hidden_v, act_v, slope_v, gate_v, up_v, acc, crecv, xbuf,
    qbuf, qpeer, qx, nq, nout, nrecv, nfar, own_t, far_t, tsend, trecv, dsend, drecv,
    load_sem, chunk_sem, ssem, rsem,
):
    g = lax.axis_index("groups")
    t = lax.axis_index("tok")
    h = lax.axis_index("head")
    n_x = n_tok // 2
    n_pair = n_head // 2
    x = t // 2
    core = lax.rem(t, 2)
    par = lax.rem(h, 2)
    pair = h // 2
    core_peer = {"tok": 2 * x + 1 - core}
    head_peer = {"head": 2 * pair + 1 - par}
    x_peers = [{"tok": 2 * lax.rem(x + d, n_x) + core} for d in range(1, n_x)]
    g_peers = [{"groups": lax.rem(g + d, n_group)} for d in range(1, n_group)]
    pair_of = [lax.rem(pair + o, n_pair) for o in range(n_pair)]
    par_peers = [{"head": 2 * pair_of[o] + par} for o in range(1, n_pair)]

    barrier = pltpu.get_barrier_semaphore()
    everyone = [core_peer, head_peer] + x_peers + g_peers + par_peers
    for peer in everyone:
        pl.semaphore_signal(barrier, inc=1, device_id=peer, device_id_type=MESH)

    sends, held = [], {}
    short = ssem.shape[0] - n_long

    def send(src, dst, peer, long=False):
        turn = sum(1 for c in sends if c[1] == long)
        slot = short + turn if long else turn % short
        if slot in held:
            held[slot].wait_send()
        copy = pltpu.make_async_remote_copy(
            src_ref=src, dst_ref=dst, send_sem=ssem.at[slot], recv_sem=rsem.at[len(sends)],
            device_id=peer, device_id_type=MESH,
        )
        copy.start()
        held[slot] = copy
        sends.append((copy, long))
        return copy

    rows = keys_h.shape[1] // chunks

    def chunk_at(i):
        return pl.ds(i * rows, rows)

    key_loads = [
        pltpu.make_async_copy(
            keys_h.at[:, chunk_at(i)], keys_v.at[:, chunk_at(i)], chunk_sem.at[0, i])
        for i in range(chunks)
    ]
    value_loads = [
        pltpu.make_async_copy(
            values_h.at[:, chunk_at(i)], values_v.at[:, chunk_at(i)], chunk_sem.at[1, i])
        for i in range(chunks)
    ]
    loads = [
        pltpu.make_async_copy(samples_h, samples_v, load_sem.at[0]),
        pltpu.make_async_copy(wq_h, wq_v, load_sem.at[1]),
        pltpu.make_async_copy(init_h.at[0], init_v, load_sem.at[2]),
        pltpu.make_async_copy(rates_h, rates_v, load_sem.at[3]),
        pltpu.make_async_copy(wo_h, wo_v, load_sem.at[4]),
    ]
    for load in [loads[2], key_loads[0], loads[3], value_loads[0]] + loads[:2]:
        load.start()
    for i in range(1, chunks):
        key_loads[i].start()
        value_loads[i].start()
    loads[4].start()

    hd = fnew.shape[2]
    half = hd // 2
    qrows = qbuf.shape[1]
    group = nq.shape[2]
    cols = wo_h.shape[1]
    near = cols - far

    loads[2].wait()
    w13[:hd] = init_v[0].T
    w13[hd:] = init_v[1].T

    pl.semaphore_wait(barrier, len(everyone))

    share = hd // n_group
    first = pl.multiple_of(share * g, 16)
    w_in = []
    if far:
        step = share // 2 if share % 32 == 0 else share
        for r in range(0, share, step):
            at = pl.ds(first + r, step)
            w_in.append((
                send(wo_h.at[at, pl.ds(0, far)], wo_far.at[at], par_peers[0], True), wo_far.at[at]))
    at = pl.ds(first, share)
    w_in.append((
        send(wo_h.at[at, pl.ds(far, near)], wo_near.at[at], head_peer, True), wo_near.at[at]))
    passed = []

    def pass_on(n):
        for _ in range(min(n, len(w_in))):
            copy, ref = w_in.pop(0)
            copy.wait_recv()
            for peer in g_peers:
                passed.append(send(ref, ref, peer, True))

    loads[3].wait()

    def store_packed(ref, lead, block):
        at = 0
        for part in pack(block):
            ref[lead + (slice(at, at + part.shape[0]),)] = part
            at += part.shape[0]

    q_x = []
    for i in range(chunks):
        key_loads[i].wait()
        value_loads[i].wait()
        at = chunk_at(i)
        k = keys_v[:, at].astype(F32)
        normed = (k * lax.rsqrt(jnp.sum(k * k, axis=0, keepdims=True) + 1e-06)).astype(BF16)
        normed_v[:, at] = normed
        pre = dot(w13[...], normed)
        gate, up = pre[:hd], pre[hd:]
        scaled_v[:, at] = (rates_v[:, at] * values_v[:, at].astype(F32)).astype(BF16)
        s = sigmoid(gate)
        a = gate * s
        hidden_v[:, at] = (a * up).astype(BF16)
        act_v[:, at] = a
        slope_v[:, at] = up * (s + a * (1.0 - s))
        if i == 0:
            loads[0].wait()
            loads[1].wait()
            queries = dot_nt(samples_v[...], wq_v[...])
            qbuf[0] = queries[:qrows]
            qbuf[1] = queries[qrows:]
            q_core = send(qbuf.at[1 - core], qpeer, core_peer)
        if i == 1:
            q_core.wait_recv()
            store_packed(qx, (x,), (qbuf[core] + qpeer[...]).astype(BF16))
            for peer in x_peers:
                q_x.append(send(qx.at[x], qx.at[x], peer))

    theirs = pl.ds(pl.multiple_of(half * (1 - core), half), half)
    mine = pl.ds(pl.multiple_of(half * core, half), half)
    c_copies, x_copies = {}, {}

    def partial(m, a, b):
        acc[m] = dot_nt(a[...], b[...])
        c_copies[m] = send(acc.at[m, theirs], crecv.at[m], core_peer)

    def chip_sum(m):
        c_copies[m].wait_recv()
        store_packed(xbuf, (m, x), (acc[m, mine, :] + crecv[m]).astype(BF16))
        x_copies[m] = [send(xbuf.at[m, x], xbuf.at[m, x], peer) for peer in x_peers]

    partial(2, hidden_v, scaled_v)
    for i in range(chunks):
        at = chunk_at(i)
        hidden_grad = dot(init_v[2], scaled_v[:, at])
        up_v[:, at] = (hidden_grad * act_v[:, at]).astype(BF16)
        gate_v[:, at] = (hidden_grad * slope_v[:, at]).astype(BF16)
        if i == chunks - 2:
            chip_sum(2)
    partial(1, normed_v, up_v)
    partial(0, normed_v, gate_v)
    chip_sum(1)
    pass_on(1)

    for c in q_x:
        c.wait_recv()

    def unpack_of(ref, lead, r):
        return unpack(lambda at, n: ref[lead + (slice(at, at + n),)].astype(F32), r, hd)

    queries = unpack_of(qx, (0,), qrows)
    for j in range(1, n_x):
        queries = queries + unpack_of(qx, (j,), qrows)
    normed_q = (
        queries * lax.rsqrt(jnp.sum(queries * queries, axis=-1, keepdims=True) + 1e-06)
    ).astype(BF16)
    for j in range(nq.shape[1]):
        nq[core, j] = normed_q[j * group : (j + 1) * group]
    q_last = send(nq.at[core], nq.at[core], core_peer)
    chip_sum(0)

    f_copies = {}

    def renorm(m):
        for c in x_copies[m]:
            c.wait_recv()
        total = unpack_of(xbuf, (m, 0), half)
        for j in range(1, n_x):
            total = total + unpack_of(xbuf, (m, j), half)
        former = init_v[m, mine, :].astype(F32)
        updated = former + total * step_scale
        factor = jnp.sqrt(
            (jnp.mean(former * former, axis=-1, keepdims=True) + 1e-05)
            / (jnp.mean(updated * updated, axis=-1, keepdims=True) + 1e-05)
        )
        fnew[0, m, mine, :] = (updated * factor).astype(BF16)
        f_copies[m] = send(fnew.at[0, m, mine], fnew.at[0, m, mine], core_peer)

    order = list(range(1, n_pair)) + [0]
    per_half = nq.shape[1]
    block = group // 2
    renorm(2)
    pass_on(len(w_in))
    q_last.wait_recv()
    renorm(1)
    normed_q = [nq[pair_of[o] // per_half, lax.rem(pair_of[o], per_half)] for o in order]
    f_copies[2].wait_recv()
    f_copies[1].wait_recv()
    ups = [dot(rows_q, fnew[0, 1]) for rows_q in normed_q]
    renorm(0)
    loads[4].wait()
    f_copies[0].wait_recv()
    quarter = pl.ds(pl.multiple_of(block // 2 * core, 16), block // 2)
    n_copies, n_far = {}, []
    for o, up, rows_q in zip(order, ups, normed_q):
        gate = dot(rows_q, fnew[0, 0])
        sample_hidden = (gate * sigmoid(gate) * up).astype(BF16)
        fast_out = dot(sample_hidden, fnew[0, 2])
        normed_out = (
            fast_out * lax.rsqrt(jnp.mean(fast_out * fast_out, axis=-1, keepdims=True) + 1e-05)
        ).astype(BF16)
        nout[o, 0] = normed_out[:block]
        nout[o, 1] = normed_out[block:]
        if far and o:
            n_far.append(send(nout.at[o, 1 - par], nfar.at[1 - par], par_peers[0]))
        n_copies[o] = send(nout.at[o, 1 - par], nrecv.at[o], head_peer)
        if far and o:
            n_far.append(
                send(nout.at[o, par, quarter], nfar.at[par, quarter], par_peers[0]))

    for o in order:
        own_t[o] = dot(nout[o, par], wo_v[:, far:])
    if far:
        far_t[1 - par] = dot(nout[0, 1 - par], wo_v[:, :far])
        far_t[par] = dot(nout[0, par], wo_v[:, :far])
    for copy in passed:
        copy.wait_recv()
    t_copies = {}

    def far_terms():
        n_far[0].wait_recv()
        dsend[...] = (far_t[1 - par] + dot(nfar[1 - par], wo_far[...])).astype(BF16)
        d_copy = send(dsend, drecv, head_peer)
        n_far[1].wait_recv()
        return d_copy, send(nfar.at[par, quarter], nfar.at[par, quarter], core_peer)

    for o in range(1, n_pair):
        n_copies[o].wait_recv()
        tsend[o - 1] = (own_t[o] + dot(nrecv[o], wo_near[...])).astype(BF16)
        t_copies[o] = send(tsend.at[o - 1], trecv.at[o - 1], par_peers[o - 1])
    if far:
        d_copy, n_core = far_terms()
    n_copies[0].wait_recv()
    mixed = own_t[0] + dot(nrecv[0], wo_near[...])
    if far:
        n_core.wait_recv()
        far_sum = far_t[par] + dot(nfar[par], wo_far[...])
        d_copy.wait_recv()
        mixed_ref[:, :far] = (far_sum + drecv[...].astype(F32)).astype(BF16)
    for o in range(1, n_pair):
        t_copies[o].wait_recv()
        mixed = mixed + trecv[o - 1].astype(F32)
    mixed_ref[:, far:] = mixed.astype(BF16)

    for c in held.values():
        c.wait_send()


def copy_out(mixed_v, fast_v, mixed_out, fast_out, sem):
    stores = [
        pltpu.make_async_copy(fast_v, fast_out, sem.at[0]),
        pltpu.make_async_copy(mixed_v, mixed_out, sem.at[1]),
    ]
    for c in stores:
        c.start()
    for c in stores:
        c.wait()


FAR = 768


def shards(n_group, n_tok, n_head, keys, values, rates, fast_init, samples, w_query, w_output):
    tokens = keys.shape[0]
    hd = fast_init.shape[2]
    chunks = 3
    srows = samples.shape[0]
    block = srows // n_head
    cols = w_output.shape[1]
    n_x, n_pair = n_tok // 2, n_head // 2
    far = FAR if n_pair == 2 else 0
    near = cols - far
    dma = pltpu.SemaphoreType.DMA
    others = max(n_pair - 1, 1)
    anywhere = pl.BlockSpec(memory_space=pl.ANY)
    vmem = pltpu.VMEM
    in_vmem = pl.BlockSpec(memory_space=vmem)
    packed = (hd // 2) * hd // 128
    qrows = srows // 2
    weights = (2 if far and (hd // n_group) % 32 == 0 else 1 if far else 0) + 1
    n_long = weights * n_group
    n_sem = 8 + 4 * (n_x - 1) + 2 * n_pair - 1 + (4 if far else 0) + n_long
    body = functools.partial(
        kernel, n_group, n_tok, n_head, far, n_long, chunks, float(tokens * n_tok) ** (-0.5)
    )
    mixed, fast_new = pl.pallas_call(
        body,
        out_shape=(vmem((block, cols), BF16), vmem((1, 3, hd, hd), BF16)),
        in_specs=[anywhere] * 7,
        out_specs=(in_vmem, in_vmem),
        scratch_shapes=[
            vmem((hd, tokens), BF16),
            vmem((hd, tokens), BF16),
            vmem((1, tokens), F32),
            vmem((3, hd, hd), BF16),
            vmem(samples.shape, BF16),
            vmem((hd, w_query.shape[0]), BF16),
            vmem(w_output.shape, BF16),
            vmem((hd, near), BF16),
            vmem((hd, far or 128), BF16),
            vmem((2 * hd, hd), BF16),
            vmem((hd, tokens), BF16),
            vmem((hd, tokens), BF16),
            vmem((hd, tokens), BF16),
            vmem((hd, tokens), F32),
            vmem((hd, tokens), F32),
            vmem((hd, tokens), BF16),
            vmem((hd, tokens), BF16),
            vmem((3, hd, hd), F32),
            vmem((3, hd // 2, hd), F32),
            vmem((3, n_x, packed, 128), BF16),
            vmem((2, qrows, hd), F32),
            vmem((qrows, hd), F32),
            vmem((n_x, qrows * hd // 128, 128), BF16),
            vmem((2, n_pair // 2, 2 * block, hd), BF16),
            vmem((n_pair, 2, block, hd), BF16),
            vmem((n_pair, block, hd), BF16),
            vmem((2, block, hd), BF16),
            vmem((n_pair, block, near), F32),
            vmem((2, block, far or 128), F32),
            vmem((others, block, near), BF16),
            vmem((others, block, near), BF16),
            vmem((block, far or 128), BF16),
            vmem((block, far or 128), BF16),
            dma((5,)),
            dma((2, chunks)),
            dma((6 + n_long,)),
            dma((n_sem,)),
        ],
        compiler_params=pltpu.CompilerParams(
            collective_id=0, has_side_effects=True, vmem_limit_bytes=60 << 20
        ),
    )(keys.T, values.T, rates.T, fast_init, samples, w_query.T, w_output)
    outs = (
        jax.ShapeDtypeStruct((block, cols), BF16),
        jax.ShapeDtypeStruct((1, 3, hd, hd), BF16),
    )
    return pl.pallas_call(
        copy_out,
        out_shape=outs,
        in_specs=[in_vmem] * 2,
        out_specs=(anywhere, anywhere),
        scratch_shapes=[dma((2,))],
    )(
        pltpu.with_memory_space_constraint(mixed, vmem),
        pltpu.with_memory_space_constraint(fast_new, vmem),
    )


def solution(mesh):
    return jax.shard_map(
        functools.partial(
            shards, mesh.shape["groups"], mesh.shape["tok"], mesh.shape["head"]
        ),
        mesh=mesh,
        in_specs=(
            P(("groups", "tok"), "head"),
            P(("groups", "tok"), "head"),
            P(("groups", "tok"), "head"),
            P("head", None, None, None),
            P("groups", "tok"),
            P("tok", "head"),
            P("head", "tok"),
        ),
        out_specs=(P(("groups", "head"), "tok"), P(("groups", "head"), None, None, None)),
        check_vma=False,
    )
```

```python
import functools

import jax
import jax.numpy as jnp
from jax import lax
from jax.experimental import pallas as pl
from jax.experimental.pallas import tpu as pltpu
from jax.sharding import PartitionSpec as P

MESH = pl.DeviceIdType.MESH
F32 = jnp.float32
BF16 = jnp.bfloat16


def dot(a, b):
    return jnp.dot(a, b, preferred_element_type=F32)


def dot_tn(a, b):
    return lax.dot_general(a, b, (((0,), (0,)), ((), ())), preferred_element_type=F32)


def dot_nt(a, b):
    return lax.dot_general(a, b, (((1,), (1,)), ((), ())), preferred_element_type=F32)


def sigmoid(v):
    return 0.5 * jnp.tanh(0.5 * v) + 0.5


def pack(block):
    r, hd = block.shape
    full = hd // 128
    parts = [block[:, 128 * i : 128 * (i + 1)] for i in range(full)]
    if hd % 128:
        tail = block[:, 128 * full :]
        parts.append(jnp.concatenate([tail[: r // 2], tail[r // 2 :]], axis=1))
    return parts


def unpack(rows_of, r, hd):
    full = hd // 128
    parts = [rows_of(i * r, r) for i in range(full)]
    tail = rows_of(full * r, r // 2)
    parts.append(jnp.concatenate([tail[:, :64], tail[:, 64:]], axis=0))
    return jnp.concatenate(parts, axis=1)


def kernel(
    n_group, n_tok, n_head, far, n_long, chunks, step_scale,
    keys_h, values_h, rates_h, init_h, samples_h, wq_h, wo_h,
    mixed_ref, fnew,
    keys_v, values_v, rates_v, init_v, samples_v, wq_v, wo_v, wo_near, wo_far,
    w13, normed_v, scaled_v, hidden_v, act_v, slope_v, gate_v, up_v, acc, csend, crecv, xbuf,
    qbuf, qpeer, qx, nq, nout, npack, nrecv, nfar, own_t, far_t, tsend, trecv, dsend, drecv,
    load_sem, chunk_sem, ssem, rsem,
):
    g = lax.axis_index("groups")
    t = lax.axis_index("tok")
    h = lax.axis_index("head")
    n_x = n_tok // 2
    n_pair = n_head // 2
    x = t // 2
    core = lax.rem(t, 2)
    par = lax.rem(h, 2)
    pair = h // 2
    core_peer = {"tok": 2 * x + 1 - core}
    head_peer = {"head": 2 * pair + 1 - par}
    x_peers = [{"tok": 2 * lax.rem(x + d, n_x) + core} for d in range(1, n_x)]
    g_peers = [{"groups": lax.rem(g + d, n_group)} for d in range(1, n_group)]
    pair_of = [lax.rem(pair + o, n_pair) for o in range(n_pair)]
    par_peers = [{"head": 2 * pair_of[o] + par} for o in range(1, n_pair)]

    barrier = pltpu.get_barrier_semaphore()
    everyone = [core_peer, head_peer] + x_peers + g_peers + par_peers
    for peer in everyone:
        pl.semaphore_signal(barrier, inc=1, device_id=peer, device_id_type=MESH)

    sends, held = [], {}
    short = ssem.shape[0] - n_long

    def send(src, dst, peer, long=False):
        turn = sum(1 for c in sends if c[1] == long)
        slot = short + turn if long else turn % short
        if slot in held:
            held[slot].wait_send()
        copy = pltpu.make_async_remote_copy(
            src_ref=src, dst_ref=dst, send_sem=ssem.at[slot], recv_sem=rsem.at[len(sends)],
            device_id=peer, device_id_type=MESH,
        )
        copy.start()
        held[slot] = copy
        sends.append((copy, long))
        return copy

    rows = keys_h.shape[1] // chunks

    def chunk_at(i):
        return pl.ds(i * rows, rows)

    key_loads = [
        pltpu.make_async_copy(
            keys_h.at[:, chunk_at(i)], keys_v.at[:, chunk_at(i)], chunk_sem.at[0, i])
        for i in range(chunks)
    ]
    value_loads = [
        pltpu.make_async_copy(
            values_h.at[:, chunk_at(i)], values_v.at[:, chunk_at(i)], chunk_sem.at[1, i])
        for i in range(chunks)
    ]
    loads = [
        pltpu.make_async_copy(samples_h, samples_v, load_sem.at[0]),
        pltpu.make_async_copy(wq_h, wq_v, load_sem.at[1]),
        pltpu.make_async_copy(init_h.at[0], init_v, load_sem.at[2]),
        pltpu.make_async_copy(rates_h, rates_v, load_sem.at[3]),
        pltpu.make_async_copy(wo_h, wo_v, load_sem.at[4]),
    ]
    for load in [loads[2], key_loads[0], loads[3], value_loads[0]] + loads[:2]:
        load.start()
    for i in range(1, chunks):
        key_loads[i].start()
        value_loads[i].start()
    loads[4].start()

    hd = fnew.shape[2]
    half = hd // 2
    qrows = qbuf.shape[1]
    group = nq.shape[2]
    cols = wo_h.shape[1]
    near = cols - far

    loads[2].wait()
    w13[:hd] = init_v[0].T
    w13[hd:] = init_v[1].T

    pl.semaphore_wait(barrier, len(everyone))

    share = hd // n_group
    first = pl.multiple_of(share * g, 16)
    w_in = []
    if far:
        step = share // 2 if share % 32 == 0 else share
        for r in range(0, share, step):
            at = pl.ds(first + r, step)
            w_in.append((
                send(wo_h.at[at, pl.ds(0, far)], wo_far.at[at], par_peers[0], True), wo_far.at[at]))
    at = pl.ds(first, share)
    w_in.append((
        send(wo_h.at[at, pl.ds(far, near)], wo_near.at[at], head_peer, True), wo_near.at[at]))
    passed = []

    def pass_on(n):
        for _ in range(min(n, len(w_in))):
            copy, ref = w_in.pop(0)
            copy.wait_recv()
            for peer in g_peers:
                passed.append(send(ref, ref, peer, True))

    loads[3].wait()

    def store_packed(ref, lead, block):
        at = 0
        for part in pack(block):
            ref[lead + (slice(at, at + part.shape[0]),)] = part
            at += part.shape[0]

    q_x = []
    for i in range(chunks):
        key_loads[i].wait()
        value_loads[i].wait()
        at = chunk_at(i)
        k = keys_v[:, at].astype(F32)
        normed = (k * lax.rsqrt(jnp.sum(k * k, axis=0, keepdims=True) + 1e-06)).astype(BF16)
        normed_v[:, at] = normed
        pre = dot(w13[...], normed)
        gate, up = pre[:hd], pre[hd:]
        scaled_v[:, at] = (rates_v[:, at] * values_v[:, at].astype(F32)).astype(BF16)
        s = sigmoid(gate)
        a = gate * s
        hidden_v[:, at] = (a * up).astype(BF16)
        act_v[:, at] = a
        slope_v[:, at] = up * (s + a * (1.0 - s))
        if i == 0:
            loads[0].wait()
            loads[1].wait()
            queries = dot_nt(samples_v[...], wq_v[...])
            qbuf[0] = queries[:qrows]
            qbuf[1] = queries[qrows:]
            q_core = send(qbuf.at[1 - core], qpeer, core_peer)
        if i == 1:
            q_core.wait_recv()
            store_packed(qx, (x,), (qbuf[core] + qpeer[...]).astype(BF16))
            for peer in x_peers:
                q_x.append(send(qx.at[x], qx.at[x], peer))

    theirs = pl.ds(pl.multiple_of(half * (1 - core), half), half)
    mine = pl.ds(pl.multiple_of(half * core, half), half)
    c_copies, x_copies = {}, {}

    def partial(m, a, b, between=None):
        if between is None:
            acc[m] = dot_nt(a[...], b[...])
        else:
            acc[m, theirs] = dot_nt(a[theirs, :], b[...])
        csend[m] = acc[m, theirs, :].astype(BF16)
        c_copies[m] = send(csend.at[m], crecv.at[m], core_peer)
        if between is not None:
            between()
            acc[m, mine] = dot_nt(a[mine, :], b[...])

    def chip_sum(m):
        c_copies[m].wait_recv()
        store_packed(xbuf, (m, x), (acc[m, mine, :] + crecv[m].astype(F32)).astype(BF16))
        x_copies[m] = [send(xbuf.at[m, x], xbuf.at[m, x], peer) for peer in x_peers]

    partial(2, hidden_v, scaled_v)
    for i in range(chunks):
        at = chunk_at(i)
        hidden_grad = dot(init_v[2], scaled_v[:, at])
        up_v[:, at] = (hidden_grad * act_v[:, at]).astype(BF16)
        gate_v[:, at] = (hidden_grad * slope_v[:, at]).astype(BF16)
        if i == chunks - 2:
            chip_sum(2)
    partial(1, normed_v, up_v)
    partial(0, normed_v, gate_v, lambda: chip_sum(1))
    chip_sum(0)
    pass_on(1)

    for c in q_x:
        c.wait_recv()

    def unpack_of(ref, lead, r):
        return unpack(lambda at, n: ref[lead + (slice(at, at + n),)].astype(F32), r, hd)

    queries = unpack_of(qx, (0,), qrows)
    for j in range(1, n_x):
        queries = queries + unpack_of(qx, (j,), qrows)
    normed_q = (
        queries * lax.rsqrt(jnp.sum(queries * queries, axis=-1, keepdims=True) + 1e-06)
    ).astype(BF16)
    for j in range(nq.shape[1]):
        nq[core, j] = normed_q[j * group : (j + 1) * group]
    q_last = send(nq.at[core], nq.at[core], core_peer)

    f_copies = {}

    def renorm(m):
        for c in x_copies[m]:
            c.wait_recv()
        total = unpack_of(xbuf, (m, 0), half)
        for j in range(1, n_x):
            total = total + unpack_of(xbuf, (m, j), half)
        former = init_v[m, mine, :].astype(F32)
        updated = former + total * step_scale
        factor = jnp.sqrt(
            (jnp.mean(former * former, axis=-1, keepdims=True) + 1e-05)
            / (jnp.mean(updated * updated, axis=-1, keepdims=True) + 1e-05)
        )
        fnew[0, m, mine, :] = (updated * factor).astype(BF16)
        f_copies[m] = send(fnew.at[0, m, mine], fnew.at[0, m, mine], core_peer)

    order = list(range(1, n_pair)) + [0]
    per_half = nq.shape[1]
    block = group // 2
    renorm(2)
    pass_on(len(w_in))
    q_last.wait_recv()
    renorm(1)
    normed_q = [nq[pair_of[o] // per_half, lax.rem(pair_of[o], per_half)] for o in order]
    f_copies[2].wait_recv()
    f_copies[1].wait_recv()
    ups = [dot(rows_q, fnew[0, 1]) for rows_q in normed_q]
    renorm(0)
    loads[4].wait()
    f_copies[0].wait_recv()
    prows = nrecv.shape[1]
    piece = pl.ds(pl.multiple_of(prows // 2 * core, 16), prows // 2)
    n_copies, n_far = {}, []
    for o, up, rows_q in zip(order, ups, normed_q):
        gate = dot(rows_q, fnew[0, 0])
        sample_hidden = (gate * sigmoid(gate) * up).astype(BF16)
        fast_out = dot(sample_hidden, fnew[0, 2])
        normed_out = (
            fast_out * lax.rsqrt(jnp.mean(fast_out * fast_out, axis=-1, keepdims=True) + 1e-05)
        ).astype(BF16)
        for q in range(2):
            nout[o, q] = normed_out[q * block : (q + 1) * block]
            store_packed(npack, (o, q), normed_out[q * block : (q + 1) * block])
        if far and o:
            n_far.append(send(npack.at[o, 1 - par], nfar.at[1 - par], par_peers[0]))
        n_copies[o] = send(npack.at[o, 1 - par], nrecv.at[o], head_peer)
        if far and o:
            n_far.append(
                send(npack.at[o, par, piece], nfar.at[par, piece], par_peers[0]))

    for o in order:
        own_t[o] = dot(nout[o, par], wo_v[:, far:])
    if far:
        far_t[1 - par] = dot(nout[0, 1 - par], wo_v[:, :far])
        far_t[par] = dot(nout[0, par], wo_v[:, :far])
    for copy in passed:
        copy.wait_recv()
    t_copies = {}

    def block_of(ref, lead):
        return unpack(lambda at, n: ref[lead + (slice(at, at + n),)], block, hd)

    def far_terms():
        n_far[0].wait_recv()
        dsend[...] = (far_t[1 - par] + dot(block_of(nfar, (1 - par,)), wo_far[...])).astype(BF16)
        d_copy = send(dsend, drecv, head_peer)
        n_far[1].wait_recv()
        return d_copy, send(nfar.at[par, piece], nfar.at[par, piece], core_peer)

    for o in range(1, n_pair):
        n_copies[o].wait_recv()
        tsend[o - 1] = (own_t[o] + dot(block_of(nrecv, (o,)), wo_near[...])).astype(BF16)
        t_copies[o] = send(tsend.at[o - 1], trecv.at[o - 1], par_peers[o - 1])
    if far:
        d_copy, n_core = far_terms()
    n_copies[0].wait_recv()
    mixed = own_t[0] + dot(block_of(nrecv, (0,)), wo_near[...])
    if far:
        n_core.wait_recv()
        far_sum = far_t[par] + dot(block_of(nfar, (par,)), wo_far[...])
        d_copy.wait_recv()
        mixed_ref[:, :far] = (far_sum + drecv[...].astype(F32)).astype(BF16)
    for o in range(1, n_pair):
        t_copies[o].wait_recv()
        mixed = mixed + trecv[o - 1].astype(F32)
    mixed_ref[:, far:] = mixed.astype(BF16)

    for c in held.values():
        c.wait_send()


def copy_out(mixed_v, fast_v, mixed_out, fast_out, sem):
    stores = [
        pltpu.make_async_copy(fast_v, fast_out, sem.at[0]),
        pltpu.make_async_copy(mixed_v, mixed_out, sem.at[1]),
    ]
    for c in stores:
        c.start()
    for c in stores:
        c.wait()


FAR = 896


def shards(n_group, n_tok, n_head, keys, values, rates, fast_init, samples, w_query, w_output):
    tokens = keys.shape[0]
    hd = fast_init.shape[2]
    chunks = 3
    srows = samples.shape[0]
    block = srows // n_head
    cols = w_output.shape[1]
    n_x, n_pair = n_tok // 2, n_head // 2
    far = FAR if n_pair == 2 else 0
    near = cols - far
    dma = pltpu.SemaphoreType.DMA
    others = max(n_pair - 1, 1)
    anywhere = pl.BlockSpec(memory_space=pl.ANY)
    vmem = pltpu.VMEM
    in_vmem = pl.BlockSpec(memory_space=vmem)
    packed = (hd // 2) * hd // 128
    qrows = srows // 2
    weights = (2 if far and (hd // n_group) % 32 == 0 else 1 if far else 0) + 1
    n_long = weights * n_group
    n_sem = 8 + 4 * (n_x - 1) + 2 * n_pair - 1 + (4 if far else 0) + n_long
    body = functools.partial(
        kernel, n_group, n_tok, n_head, far, n_long, chunks, float(tokens * n_tok) ** (-0.5)
    )
    mixed, fast_new = pl.pallas_call(
        body,
        out_shape=(vmem((block, cols), BF16), vmem((1, 3, hd, hd), BF16)),
        in_specs=[anywhere] * 7,
        out_specs=(in_vmem, in_vmem),
        scratch_shapes=[
            vmem((hd, tokens), BF16),
            vmem((hd, tokens), BF16),
            vmem((1, tokens), F32),
            vmem((3, hd, hd), BF16),
            vmem(samples.shape, BF16),
            vmem((hd, w_query.shape[0]), BF16),
            vmem(w_output.shape, BF16),
            vmem((hd, near), BF16),
            vmem((hd, far or 128), BF16),
            vmem((2 * hd, hd), BF16),
            vmem((hd, tokens), BF16),
            vmem((hd, tokens), BF16),
            vmem((hd, tokens), BF16),
            vmem((hd, tokens), F32),
            vmem((hd, tokens), F32),
            vmem((hd, tokens), BF16),
            vmem((hd, tokens), BF16),
            vmem((3, hd, hd), F32),
            vmem((3, hd // 2, hd), BF16),
            vmem((3, hd // 2, hd), BF16),
            vmem((3, n_x, packed, 128), BF16),
            vmem((2, qrows, hd), F32),
            vmem((qrows, hd), F32),
            vmem((n_x, qrows * hd // 128, 128), BF16),
            vmem((2, n_pair // 2, 2 * block, hd), BF16),
            vmem((n_pair, 2, block, hd), BF16),
            vmem((n_pair, 2, block * hd // 128, 128), BF16),
            vmem((n_pair, block * hd // 128, 128), BF16),
            vmem((2, block * hd // 128, 128), BF16),
            vmem((n_pair, block, near), F32),
            vmem((2, block, far or 128), F32),
            vmem((others, block, near), BF16),
            vmem((others, block, near), BF16),
            vmem((block, far or 128), BF16),
            vmem((block, far or 128), BF16),
            dma((5,)),
            dma((2, chunks)),
            dma((6 + n_long,)),
            dma((n_sem,)),
        ],
        compiler_params=pltpu.CompilerParams(
            collective_id=0, has_side_effects=True, vmem_limit_bytes=60 << 20
        ),
    )(keys.T, values.T, rates.T, fast_init, samples, w_query.T, w_output)
    outs = (
        jax.ShapeDtypeStruct((block, cols), BF16),
        jax.ShapeDtypeStruct((1, 3, hd, hd), BF16),
    )
    return pl.pallas_call(
        copy_out,
        out_shape=outs,
        in_specs=[in_vmem] * 2,
        out_specs=(anywhere, anywhere),
        scratch_shapes=[dma((2,))],
    )(
        pltpu.with_memory_space_constraint(mixed, vmem),
        pltpu.with_memory_space_constraint(fast_new, vmem),
    )


def solution(mesh):
    return jax.shard_map(
        functools.partial(
            shards, mesh.shape["groups"], mesh.shape["tok"], mesh.shape["head"]
        ),
        mesh=mesh,
        in_specs=(
            P(("groups", "tok"), "head"),
            P(("groups", "tok"), "head"),
            P(("groups", "tok"), "head"),
            P("head", None, None, None),
            P("groups", "tok"),
            P("tok", "head"),
            P("head", "tok"),
        ),
        out_specs=(P(("groups", "head"), "tok"), P(("groups", "head"), None, None, None)),
        check_vma=False,
    )
```

```python
import functools

import jax
import jax.numpy as jnp
from jax import lax
from jax.experimental import pallas as pl
from jax.experimental.pallas import tpu as pltpu
from jax.sharding import PartitionSpec as P

MESH = pl.DeviceIdType.MESH
F32 = jnp.float32
BF16 = jnp.bfloat16


def dot(a, b):
    return jnp.dot(a, b, preferred_element_type=F32)


def dot_tn(a, b):
    return lax.dot_general(a, b, (((0,), (0,)), ((), ())), preferred_element_type=F32)


def dot_nt(a, b):
    return lax.dot_general(a, b, (((1,), (1,)), ((), ())), preferred_element_type=F32)


def sigmoid(v):
    return 0.5 * jnp.tanh(0.5 * v) + 0.5


def pack(block):
    r, hd = block.shape
    full = hd // 128
    parts = [block[:, 128 * i : 128 * (i + 1)] for i in range(full)]
    if hd % 128:
        tail = block[:, 128 * full :]
        parts.append(jnp.concatenate([tail[: r // 2], tail[r // 2 :]], axis=1))
    return parts


def unpack(rows_of, r, hd):
    full = hd // 128
    parts = [rows_of(i * r, r) for i in range(full)]
    tail = rows_of(full * r, r // 2)
    parts.append(jnp.concatenate([tail[:, :64], tail[:, 64:]], axis=0))
    return jnp.concatenate(parts, axis=1)


def kernel(
    n_group, n_tok, n_head, far, n_long, chunks, step_scale,
    keys_h, values_h, rates_h, init_h, samples_h, wq_h, wo_h,
    mixed_ref, fnew,
    keys_v, values_v, rates_v, init_v, samples_v, wq_v, wo_v, wo_near, wo_far,
    w13, normed_v, scaled_v, hidden_v, act_v, slope_v, gate_v, up_v, acc, csend, crecv, xbuf,
    qbuf, qpeer, qx, nq, nout, npack, nrecv, nfar, own_t, far_t, tsend, trecv, dsend, drecv,
    load_sem, chunk_sem, ssem, rsem,
):
    g = lax.axis_index("groups")
    t = lax.axis_index("tok")
    h = lax.axis_index("head")
    n_x = n_tok // 2
    n_pair = n_head // 2
    x = t // 2
    core = lax.rem(t, 2)
    par = lax.rem(h, 2)
    pair = h // 2
    core_peer = {"tok": 2 * x + 1 - core}
    head_peer = {"head": 2 * pair + 1 - par}
    x_peers = [{"tok": 2 * lax.rem(x + d, n_x) + core} for d in range(1, n_x)]
    g_peers = [{"groups": lax.rem(g + d, n_group)} for d in range(1, n_group)]
    pair_of = [lax.rem(pair + o, n_pair) for o in range(n_pair)]
    par_peers = [{"head": 2 * pair_of[o] + par} for o in range(1, n_pair)]

    barrier = pltpu.get_barrier_semaphore()
    everyone = [core_peer, head_peer] + x_peers + g_peers + par_peers
    for peer in everyone:
        pl.semaphore_signal(barrier, inc=1, device_id=peer, device_id_type=MESH)

    sends, held = [], {}
    short = ssem.shape[0] - n_long

    def send(src, dst, peer, long=False):
        turn = sum(1 for c in sends if c[1] == long)
        slot = short + turn if long else turn % short
        if slot in held:
            held[slot].wait_send()
        copy = pltpu.make_async_remote_copy(
            src_ref=src, dst_ref=dst, send_sem=ssem.at[slot], recv_sem=rsem.at[len(sends)],
            device_id=peer, device_id_type=MESH,
        )
        copy.start()
        held[slot] = copy
        sends.append((copy, long))
        return copy

    rows = keys_h.shape[1] // chunks

    def chunk_at(i):
        return pl.ds(i * rows, rows)

    key_loads = [
        pltpu.make_async_copy(
            keys_h.at[:, chunk_at(i)], keys_v.at[:, chunk_at(i)], chunk_sem.at[0, i])
        for i in range(chunks)
    ]
    value_loads = [
        pltpu.make_async_copy(
            values_h.at[:, chunk_at(i)], values_v.at[:, chunk_at(i)], chunk_sem.at[1, i])
        for i in range(chunks)
    ]
    loads = [
        pltpu.make_async_copy(samples_h, samples_v, load_sem.at[0]),
        pltpu.make_async_copy(wq_h, wq_v, load_sem.at[1]),
        pltpu.make_async_copy(init_h.at[0], init_v, load_sem.at[2]),
        pltpu.make_async_copy(rates_h, rates_v, load_sem.at[3]),
        pltpu.make_async_copy(wo_h, wo_v, load_sem.at[4]),
    ]
    for load in [loads[2], key_loads[0], loads[3], value_loads[0]] + loads[:2]:
        load.start()
    for i in range(1, chunks):
        key_loads[i].start()
        value_loads[i].start()
    loads[4].start()

    hd = fnew.shape[2]
    half = hd // 2
    qrows = qbuf.shape[1]
    group = nq.shape[2]
    cols = wo_h.shape[1]
    near = cols - far

    loads[2].wait()
    w13[:hd] = init_v[0].T
    w13[hd:] = init_v[1].T

    pl.semaphore_wait(barrier, len(everyone))

    share = hd // n_group
    first = pl.multiple_of(share * g, 16)
    w_in = []
    at = pl.ds(first, share)
    w_in.append((
        send(wo_h.at[at, pl.ds(far, near)], wo_near.at[at], head_peer, True), wo_near.at[at]))
    if far:
        step = share // 2 if share % 32 == 0 else share
        for r in range(0, share, step):
            at = pl.ds(first + r, step)
            w_in.append((
                send(wo_h.at[at, pl.ds(0, far)], wo_far.at[at], par_peers[0], True), wo_far.at[at]))
    passed = []

    def pass_on(n):
        for _ in range(min(n, len(w_in))):
            copy, ref = w_in.pop(0)
            copy.wait_recv()
            for peer in g_peers:
                passed.append(send(ref, ref, peer, True))

    loads[3].wait()

    def store_packed(ref, lead, block):
        at = 0
        for part in pack(block):
            ref[lead + (slice(at, at + part.shape[0]),)] = part
            at += part.shape[0]

    q_x = []
    for i in range(chunks):
        key_loads[i].wait()
        value_loads[i].wait()
        at = chunk_at(i)
        k = keys_v[:, at].astype(F32)
        normed = (k * lax.rsqrt(jnp.sum(k * k, axis=0, keepdims=True) + 1e-06)).astype(BF16)
        normed_v[:, at] = normed
        pre = dot(w13[...], normed)
        gate, up = pre[:hd], pre[hd:]
        scaled_v[:, at] = (rates_v[:, at] * values_v[:, at].astype(F32)).astype(BF16)
        s = sigmoid(gate)
        a = gate * s
        hidden_v[:, at] = (a * up).astype(BF16)
        act_v[:, at] = a
        slope_v[:, at] = up * (s + a * (1.0 - s))
        if i == 0:
            loads[0].wait()
            loads[1].wait()
            queries = dot_nt(samples_v[...], wq_v[...])
            qbuf[0] = queries[:qrows]
            qbuf[1] = queries[qrows:]
            q_core = send(qbuf.at[1 - core], qpeer, core_peer)
        if i == 1:
            q_core.wait_recv()
            store_packed(qx, (x,), (qbuf[core] + qpeer[...]).astype(BF16))
            for peer in x_peers:
                q_x.append(send(qx.at[x], qx.at[x], peer))

    theirs = pl.ds(pl.multiple_of(half * (1 - core), half), half)
    mine = pl.ds(pl.multiple_of(half * core, half), half)
    c_copies, x_copies = {}, {}

    def partial(m, a, b, between=None):
        if between is None:
            acc[m] = dot_nt(a[...], b[...])
        else:
            acc[m, theirs] = dot_nt(a[theirs, :], b[...])
        csend[m] = acc[m, theirs, :].astype(BF16)
        c_copies[m] = send(csend.at[m], crecv.at[m], core_peer)
        if between is not None:
            between()
            acc[m, mine] = dot_nt(a[mine, :], b[...])

    def chip_sum(m):
        c_copies[m].wait_recv()
        store_packed(xbuf, (m, x), (acc[m, mine, :] + crecv[m].astype(F32)).astype(BF16))
        x_copies[m] = [send(xbuf.at[m, x], xbuf.at[m, x], peer) for peer in x_peers]

    partial(2, hidden_v, scaled_v)
    for i in range(chunks):
        at = chunk_at(i)
        hidden_grad = dot(init_v[2], scaled_v[:, at])
        up_v[:, at] = (hidden_grad * act_v[:, at]).astype(BF16)
        gate_v[:, at] = (hidden_grad * slope_v[:, at]).astype(BF16)
        if i == chunks - 2:
            chip_sum(2)
    partial(1, normed_v, up_v)
    partial(0, normed_v, gate_v, lambda: chip_sum(1))
    chip_sum(0)
    pass_on(1)

    for c in q_x:
        c.wait_recv()

    def unpack_of(ref, lead, r):
        return unpack(lambda at, n: ref[lead + (slice(at, at + n),)].astype(F32), r, hd)

    queries = unpack_of(qx, (0,), qrows)
    for j in range(1, n_x):
        queries = queries + unpack_of(qx, (j,), qrows)
    normed_q = (
        queries * lax.rsqrt(jnp.sum(queries * queries, axis=-1, keepdims=True) + 1e-06)
    ).astype(BF16)
    for j in range(nq.shape[1]):
        nq[core, j] = normed_q[j * group : (j + 1) * group]
    q_last = send(nq.at[core], nq.at[core], core_peer)

    f_copies = {}

    def renorm(m):
        for c in x_copies[m]:
            c.wait_recv()
        total = unpack_of(xbuf, (m, 0), half)
        for j in range(1, n_x):
            total = total + unpack_of(xbuf, (m, j), half)
        former = init_v[m, mine, :].astype(F32)
        updated = former + total * step_scale
        factor = jnp.sqrt(
            (jnp.mean(former * former, axis=-1, keepdims=True) + 1e-05)
            / (jnp.mean(updated * updated, axis=-1, keepdims=True) + 1e-05)
        )
        fnew[0, m, mine, :] = (updated * factor).astype(BF16)
        f_copies[m] = send(fnew.at[0, m, mine], fnew.at[0, m, mine], core_peer)

    order = list(range(1, n_pair)) + [0]
    per_half = nq.shape[1]
    block = group // 2
    renorm(2)
    pass_on(len(w_in))
    q_last.wait_recv()
    renorm(1)
    normed_q = [nq[pair_of[o] // per_half, lax.rem(pair_of[o], per_half)] for o in order]
    f_copies[2].wait_recv()
    f_copies[1].wait_recv()
    ups = [dot(rows_q, fnew[0, 1]) for rows_q in normed_q]
    renorm(0)
    loads[4].wait()
    f_copies[0].wait_recv()
    prows = nrecv.shape[1]
    piece = pl.ds(pl.multiple_of(prows // 2 * core, 16), prows // 2)
    n_copies, n_far = {}, []
    for o, up, rows_q in zip(order, ups, normed_q):
        gate = dot(rows_q, fnew[0, 0])
        sample_hidden = (gate * sigmoid(gate) * up).astype(BF16)
        fast_out = dot(sample_hidden, fnew[0, 2])
        normed_out = (
            fast_out * lax.rsqrt(jnp.mean(fast_out * fast_out, axis=-1, keepdims=True) + 1e-05)
        ).astype(BF16)
        for q in range(2):
            nout[o, q] = normed_out[q * block : (q + 1) * block]
            store_packed(npack, (o, q), normed_out[q * block : (q + 1) * block])
        if far and o:
            n_far.append(send(npack.at[o, 1 - par], nfar.at[1 - par], par_peers[0]))
        n_copies[o] = send(npack.at[o, 1 - par], nrecv.at[o], head_peer)
        if far and o:
            n_far.append(
                send(npack.at[o, par, piece], nfar.at[par, piece], par_peers[0]))

    for o in order:
        own_t[o] = dot(nout[o, par], wo_v[:, far:])
    if far:
        far_t[1 - par] = dot(nout[0, 1 - par], wo_v[:, :far])
        far_t[par] = dot(nout[0, par], wo_v[:, :far])
    for copy in passed:
        copy.wait_recv()
    t_copies = {}

    def block_of(ref, lead):
        return unpack(lambda at, n: ref[lead + (slice(at, at + n),)], block, hd)

    def far_terms():
        n_far[0].wait_recv()
        dsend[...] = (far_t[1 - par] + dot(block_of(nfar, (1 - par,)), wo_far[...])).astype(BF16)
        d_copy = send(dsend, drecv, head_peer)
        n_far[1].wait_recv()
        return d_copy, send(nfar.at[par, piece], nfar.at[par, piece], core_peer)

    for o in range(1, n_pair):
        n_copies[o].wait_recv()
        tsend[o - 1] = (own_t[o] + dot(block_of(nrecv, (o,)), wo_near[...])).astype(BF16)
        t_copies[o] = send(tsend.at[o - 1], trecv.at[o - 1], par_peers[o - 1])
    if far:
        d_copy, n_core = far_terms()
    n_copies[0].wait_recv()
    mixed = own_t[0] + dot(block_of(nrecv, (0,)), wo_near[...])
    if far:
        n_core.wait_recv()
        far_sum = far_t[par] + dot(block_of(nfar, (par,)), wo_far[...])
        d_copy.wait_recv()
        mixed_ref[:, :far] = (far_sum + drecv[...].astype(F32)).astype(BF16)
    for o in range(1, n_pair):
        t_copies[o].wait_recv()
        mixed = mixed + trecv[o - 1].astype(F32)
    mixed_ref[:, far:] = mixed.astype(BF16)

    for c in held.values():
        c.wait_send()


def copy_out(mixed_v, fast_v, mixed_out, fast_out, sem):
    stores = [
        pltpu.make_async_copy(fast_v, fast_out, sem.at[0]),
        pltpu.make_async_copy(mixed_v, mixed_out, sem.at[1]),
    ]
    for c in stores:
        c.start()
    for c in stores:
        c.wait()


FAR = 896


def shards(n_group, n_tok, n_head, keys, values, rates, fast_init, samples, w_query, w_output):
    tokens = keys.shape[0]
    hd = fast_init.shape[2]
    chunks = 3
    srows = samples.shape[0]
    block = srows // n_head
    cols = w_output.shape[1]
    n_x, n_pair = n_tok // 2, n_head // 2
    far = FAR if n_pair == 2 else 0
    near = cols - far
    dma = pltpu.SemaphoreType.DMA
    others = max(n_pair - 1, 1)
    anywhere = pl.BlockSpec(memory_space=pl.ANY)
    vmem = pltpu.VMEM
    in_vmem = pl.BlockSpec(memory_space=vmem)
    packed = (hd // 2) * hd // 128
    qrows = srows // 2
    weights = (2 if far and (hd // n_group) % 32 == 0 else 1 if far else 0) + 1
    n_long = weights * n_group
    n_sem = 8 + 4 * (n_x - 1) + 2 * n_pair - 1 + (4 if far else 0) + n_long
    body = functools.partial(
        kernel, n_group, n_tok, n_head, far, n_long, chunks, float(tokens * n_tok) ** (-0.5)
    )
    mixed, fast_new = pl.pallas_call(
        body,
        out_shape=(vmem((block, cols), BF16), vmem((1, 3, hd, hd), BF16)),
        in_specs=[anywhere] * 7,
        out_specs=(in_vmem, in_vmem),
        scratch_shapes=[
            vmem((hd, tokens), BF16),
            vmem((hd, tokens), BF16),
            vmem((1, tokens), F32),
            vmem((3, hd, hd), BF16),
            vmem(samples.shape, BF16),
            vmem((hd, w_query.shape[0]), BF16),
            vmem(w_output.shape, BF16),
            vmem((hd, near), BF16),
            vmem((hd, far or 128), BF16),
            vmem((2 * hd, hd), BF16),
            vmem((hd, tokens), BF16),
            vmem((hd, tokens), BF16),
            vmem((hd, tokens), BF16),
            vmem((hd, tokens), F32),
            vmem((hd, tokens), F32),
            vmem((hd, tokens), BF16),
            vmem((hd, tokens), BF16),
            vmem((3, hd, hd), F32),
            vmem((3, hd // 2, hd), BF16),
            vmem((3, hd // 2, hd), BF16),
            vmem((3, n_x, packed, 128), BF16),
            vmem((2, qrows, hd), F32),
            vmem((qrows, hd), F32),
            vmem((n_x, qrows * hd // 128, 128), BF16),
            vmem((2, n_pair // 2, 2 * block, hd), BF16),
            vmem((n_pair, 2, block, hd), BF16),
            vmem((n_pair, 2, block * hd // 128, 128), BF16),
            vmem((n_pair, block * hd // 128, 128), BF16),
            vmem((2, block * hd // 128, 128), BF16),
            vmem((n_pair, block, near), F32),
            vmem((2, block, far or 128), F32),
            vmem((others, block, near), BF16),
            vmem((others, block, near), BF16),
            vmem((block, far or 128), BF16),
            vmem((block, far or 128), BF16),
            dma((5,)),
            dma((2, chunks)),
            dma((6 + n_long,)),
            dma((n_sem,)),
        ],
        compiler_params=pltpu.CompilerParams(
            collective_id=0, has_side_effects=True, vmem_limit_bytes=60 << 20
        ),
    )(keys.T, values.T, rates.T, fast_init, samples, w_query.T, w_output)
    outs = (
        jax.ShapeDtypeStruct((block, cols), BF16),
        jax.ShapeDtypeStruct((1, 3, hd, hd), BF16),
    )
    return pl.pallas_call(
        copy_out,
        out_shape=outs,
        in_specs=[in_vmem] * 2,
        out_specs=(anywhere, anywhere),
        scratch_shapes=[dma((2,))],
    )(
        pltpu.with_memory_space_constraint(mixed, vmem),
        pltpu.with_memory_space_constraint(fast_new, vmem),
    )


def solution(mesh):
    return jax.shard_map(
        functools.partial(
            shards, mesh.shape["groups"], mesh.shape["tok"], mesh.shape["head"]
        ),
        mesh=mesh,
        in_specs=(
            P(("groups", "tok"), "head"),
            P(("groups", "tok"), "head"),
            P(("groups", "tok"), "head"),
            P("head", None, None, None),
            P("groups", "tok"),
            P("tok", "head"),
            P("head", "tok"),
        ),
        out_specs=(P(("groups", "head"), "tok"), P(("groups", "head"), None, None, None)),
        check_vma=False,
    )
```
